512 devices in a mesh: comp: 64 (over z_lo, y, core), grp: 8 (over z_hi, x).
Axes of the slice: x: 4, y: 8, z: 8 (z_hi: 2, z_lo: 4; z = z_hi * 4 + z_lo), core: 2. Of those that a mesh axis runs over, the one named last changes fastest.
Arguments:
- spectrum: float32 [1152, 64, 1024], P('comp', 'grp'), may hold values from 0.1 to 1
- group_speed: float32 [2, 1152], replicated, may hold values from -0.25 to 0.25
- sea_mask: int32 [64, 1024], P('grp'), may hold values 0 or 1
- quad_index: int32 [4, 1152], replicated, may hold values from 0 to 1151
- coupling: bfloat16 [1152, 1152], replicated, may hold values from -0.1875 to 0.1875
- stokes_kernel: float32 [32, 1152], replicated, may hold values from -0.1875 to 0.1875
- ocean_flow: float32 [2, 16, 64, 1024], P(None, None, None, 'comp'), may hold values from -4 to 4
Outputs:
- forecast: float32 [1152, 64, 1024], P('comp', 'grp')
- ocean_state: float32 [2, 16, 64, 1024], P(None, None, None, 'comp')
The draws below stay inside these ranges and needn't reach their ends.
All inputs are finite; a program needn't handle non-finite values. No bound on the sum of `sea_mask` on one device may be relied on, other than what follows from the above.
Results may differ from the reference program's by a relative error of at most 0.0004.
Values sent between devices are 32-bit elements; how exact they have to be, the bound alone decides.
No kernel may reach another device: no remote copies, remote signals or barrier semaphores. Data moves between devices by JAX's collectives and lax.ppermute only.
A program may use at most 64 MiB of HBM per device.

```python
import math
import jax
import jax.numpy as jnp
from jax import lax

K = 1152
Q = 1152
L = 16
STEPS = 2
SUB = 3
NY = 64
NX = 1024


def touch_ends(values, stream_key, least, largest):
    dims = values.shape
    index_at = [jax.random.randint(jax.random.fold_in(stream_key, axis), (), 0, dims[axis]) for axis in range(len(dims))]
    values = values.at[tuple(index_at)].set(least)
    longest = dims.index(max(dims))
    index_at[longest] = (index_at[longest] + 1) % dims[longest]
    return values.at[tuple(index_at)].set(largest)


def block_levels(stream_key, shape, pieces, low, largest):
    gain, own = 1.0, jax.random.fold_in(stream_key, 6)
    for dim, parts in pieces:
        heights = jnp.exp(jax.random.uniform(jax.random.fold_in(own, dim), (parts,), jnp.float32, low / len(pieces), largest / len(pieces)))
        gain = gain * jnp.repeat(heights, shape[dim] // parts).reshape([-1 if axis == dim else 1 for axis in range(len(shape))])
    return gain


def centred(stream_key, dims, width, most, cuts=(), dtype=jnp.bfloat16):
    factor_of = block_levels(stream_key, dims, cuts, -0.22, 0.18) if cuts else 1.0
    drawn = jax.random.normal(stream_key, dims, jnp.float32) * width * factor_of
    return jnp.minimum(jnp.maximum(drawn, -most), most).astype(dtype)


def setup_inputs(seed: int = 0) -> dict:
    splits = jax.random.split(jax.random.key(seed), 8)
    spectrum = jnp.clip(jnp.exp(math.log(1.0) - 2.3025851 * jax.random.uniform(splits[0], (K, NY, NX), jnp.float32) ** block_levels(splits[0], (K, NY, NX), ((0, 64), (1, 8)), -0.2, 0.2)), 0.1, 1.0)
    group_speed = jnp.clip(jax.random.uniform(splits[1], (2, K), jnp.float32, -0.25, 0.25), -0.25, 0.25)
    sea_mask = touch_ends((jax.random.randint(splits[2], (NY, NX), 0, 5) < 4).astype(jnp.int32), jax.random.fold_in(splits[2], 1), 0, 1)
    quad_index = touch_ends(jax.random.randint(splits[3], (4, Q), 0, K), jax.random.fold_in(splits[3], 1), 0, K - 1).astype(jnp.int32)
    coupling = centred(splits[4], (K, Q), Q ** -0.5, 0.1875)
    stokes_kernel = centred(splits[5], (2 * L, K), K ** -0.5, 0.1875, (), jnp.float32)
    ocean_flow = centred(splits[6], (2, L, NY, NX), 1.0, 4.0, ((3, 64),), jnp.float32)
    return {"spectrum": spectrum, "group_speed": group_speed, "sea_mask": sea_mask, "quad_index": quad_index, "coupling": coupling, "stokes_kernel": stokes_kernel, "ocean_flow": ocean_flow}


SOURCE_GAIN = 0.3
CURRENT_GAIN = 0.25
CORIOLIS = 0.3
VISCOSITY = 0.15
MIXING = 0.15


def upwind(padded, energy, speed_x, speed_y, wet_cells):
    westward = padded[:, 1:-1, :-2]
    eastward = padded[:, 1:-1, 2:]
    southward = padded[:, :-2, 1:-1]
    northward = padded[:, 2:, 1:-1]
    moved = (energy - jnp.maximum(speed_x, 0.0) * (energy - westward)
             - jnp.minimum(speed_x, 0.0) * (eastward - energy)
             - jnp.maximum(speed_y, 0.0) * (energy - southward)
             - jnp.minimum(speed_y, 0.0) * (northward - energy))
    return moved * wet_cells


def sources(columns, quad_index, coupling, wet_flat):
    for substep in range(SUB):
        first = jnp.take(columns, quad_index[0], axis=0)
        second = jnp.take(columns, quad_index[1], axis=0)
        third = jnp.take(columns, quad_index[2], axis=0)
        fourth = jnp.take(columns, quad_index[3], axis=0)
        interaction = (first * second * (third + fourth) - third * fourth * (first + second)).astype(jnp.bfloat16)
        growth = jnp.dot(coupling, interaction, preferred_element_type=jnp.float32)
        columns = columns + wet_flat * (SOURCE_GAIN * growth / (1.0 + SOURCE_GAIN * jnp.abs(growth)))
    return columns


def laplace(padded, field):
    return padded[:, 1:-1, 2:] + padded[:, 1:-1, :-2] + padded[:, 2:, 1:-1] + padded[:, :-2, 1:-1] - 4.0 * field


def vertical(field):
    stacked = jnp.pad(field, ((1, 1), (0, 0), (0, 0)))
    return stacked[2:] + stacked[:-2] - 2.0 * field


def ocean_step(padded, flow, stokes):
    flow_x = flow[0]
    flow_y = flow[1]
    padded_x = padded[0]
    padded_y = padded[1]
    vortex = 0.5 * (padded_y[:, 1:-1, 2:] - padded_y[:, 1:-1, :-2]) - 0.5 * (padded_x[:, 2:, 1:-1] - padded_x[:, :-2, 1:-1])
    drift_x = stokes[0]
    drift_y = stokes[1]
    new_x = flow_x + CORIOLIS * (flow_y + drift_y) + vortex * drift_y + VISCOSITY * laplace(padded_x, flow_x) + MIXING * vertical(flow_x)
    new_y = flow_y - CORIOLIS * (flow_x + drift_x) - vortex * drift_x + VISCOSITY * laplace(padded_y, flow_y) + MIXING * vertical(flow_y)
    return jnp.stack([new_x, new_y])


def reference(spectrum, group_speed, sea_mask, quad_index, coupling, stokes_kernel, ocean_flow):
    wet_cells = (sea_mask == 1).astype(jnp.float32)
    energy = spectrum
    flow = ocean_flow
    for iteration in range(STEPS):
        drift = CURRENT_GAIN * jnp.tanh(flow[:, 0])
        speed_x = group_speed[0][:, None, None] + drift[0][None]
        speed_y = group_speed[1][:, None, None] + drift[1][None]
        padded = jnp.pad(energy, ((0, 0), (1, 1), (1, 1)))
        energy = upwind(padded, energy, speed_x, speed_y, wet_cells[None])

        def per_row(pair):
            row_energy, row_wet = pair
            updated = sources(row_energy, quad_index, coupling, row_wet[None])
            profile = jnp.dot(stokes_kernel, updated, precision=lax.Precision.HIGHEST)
            return updated, profile

        rows_first = jnp.transpose(energy, (1, 0, 2))
        updated, profiles = lax.map(per_row, (rows_first, wet_cells))
        energy = jnp.transpose(updated, (1, 0, 2))
        stokes = jnp.transpose(profiles, (1, 0, 2)).reshape(2, L, NY, NX)
        padded_flow = jnp.pad(flow, ((0, 0), (0, 0), (1, 1), (1, 1)))
        flow = ocean_step(padded_flow, flow, stokes)
    return energy, flow
```

```python
import functools

import jax
import jax.numpy as jnp
from jax import lax
from jax.experimental import pallas as pl
from jax.experimental.pallas import tpu as pltpu
from jax.sharding import PartitionSpec as P

L = 16
STEPS = 2
SUB = 3

SOURCE_GAIN = 0.3
CURRENT_GAIN = 0.25
CORIOLIS = 0.3
VISCOSITY = 0.15
MIXING = 0.15

ROWS = 8
COLS = 16
LANES = 128
FIELDS = 2 * L

VMEM = pl.BlockSpec(memory_space=pltpu.VMEM)
SMEM = pl.BlockSpec(memory_space=pltpu.SMEM)
SMALL = pltpu.CompilerParams(vmem_limit_bytes=16 * 2**20)


def roll(x, shift, axis=1):
    shift %= x.shape[axis]
    return pltpu.roll(x, shift, axis) if shift else x


def lane_places():
    lane = lax.broadcasted_iota(jnp.int32, (8, LANES), 1)
    return lane // COLS, lane % COLS


def exchange_blocks(x):
    sub = lax.broadcasted_iota(jnp.int32, (8, LANES), 0)
    block, _ = lane_places()
    for bit in (1, 2, 4):
        in_sub = (sub & bit) != 0
        in_block = (block & bit) != 0
        up = roll(roll(x, -bit, 0), bit * COLS)
        down = roll(roll(x, bit, 0), -bit * COLS)
        x = jnp.where(in_sub == in_block, x, jnp.where(in_block, up, down))
    return x


def to_points_kernel(x_ref, o_ref):
    parts = x_ref.shape[0]

    def one(k, carry):
        for j in range(x_ref.shape[2] // LANES):
            tile = exchange_blocks(x_ref[k, :, j * LANES : (j + 1) * LANES])
            o_ref[pl.ds(j * 8 * parts + k, 8, stride=parts), :] = tile
        return carry

    lax.fori_loop(0, parts, one, 0)


def from_points_kernel(x_ref, o_ref):
    parts = o_ref.shape[0]

    def one(k, carry):
        for j in range(o_ref.shape[2] // LANES):
            tile = x_ref[pl.ds(j * 8 * parts + k, 8, stride=parts), :]
            o_ref[k, :, j * LANES : (j + 1) * LANES] = exchange_blocks(tile)
        return carry

    lax.fori_loop(0, parts, one, 0)


def tile_rows(start, count=8):
    return pl.ds(start if isinstance(start, int) else pl.multiple_of(start, 8), count)


def pack_group(load, count, m, up_ref, down_ref, east_ref, west_ref):
    block, col = lane_places()
    east = west = None
    for h in range((count + 7) // 8):
        up = down = None
        for i in range(min(8, count - 8 * h)):
            n = 8 * h + i
            tile = load(n)
            u = roll(tile, (i - (ROWS - 1)) * COLS)
            d = roll(tile, i * COLS)
            e = roll(tile, n - (COLS - 1))
            w = roll(tile, n)
            up = u if up is None else jnp.where(block == i, u, up)
            down = d if down is None else jnp.where(block == i, d, down)
            east = e if east is None else jnp.where(col == n, e, east)
            west = w if west is None else jnp.where(col == n, w, west)
        up_ref[tile_rows((2 * m + h) * 8), :] = up
        down_ref[tile_rows((2 * m + h) * 8), :] = down
    east_ref[tile_rows(m * 8), :] = east
    west_ref[tile_rows(m * 8), :] = west


def pack_all(e_ref, f_ref, channels, edges):
    def one(m, carry):
        pack_group(lambda n: e_ref[tile_rows(m * 128 + n * 8), :], 16, m, *edges)
        return carry

    lax.fori_loop(0, channels // 128, one, 0)
    pack_group(lambda n: f_ref[n * 8 : n * 8 + 8, :], FIELDS // 8, channels // 128, *edges)


def neighbours(tile, n, m, south_ref, north_ref, west_ref, east_ref):
    block, col = lane_places()
    h, i = divmod(n, 8)
    south = roll(south_ref[tile_rows((2 * m + h) * 8), :], -i * COLS)
    north = roll(north_ref[tile_rows((2 * m + h) * 8), :], (ROWS - 1 - i) * COLS)
    west = roll(west_ref[tile_rows(m * 8), :], -n)
    east = roll(east_ref[tile_rows(m * 8), :], COLS - 1 - n)
    return (
        jnp.where(col == 0, west, roll(tile, 1)),
        jnp.where(col == COLS - 1, east, roll(tile, -1)),
        jnp.where(block == 0, south, roll(tile, COLS)),
        jnp.where(block == ROWS - 1, north, roll(tile, -COLS)),
    )


def edges_kernel(e_ref, f_ref, *edges):
    pack_all(e_ref, f_ref, e_ref.shape[0], edges)


def step_kernel(
    last,
    index_ref,
    e_in_ref,
    f_in_ref,
    wet_ref,
    speed_ref,
    coupling_ref,
    profile_ref,
    south_ref,
    north_ref,
    west_ref,
    east_ref,
    e_out_ref,
    f_out_ref,
    *rest,
):
    edges, (e_ref, inter_ref) = rest[:-2], rest[-2:]
    channels = e_in_ref.shape[0]
    quads = inter_ref.shape[0]
    halos = (south_ref, north_ref, west_ref, east_ref)
    wet = jnp.broadcast_to(wet_ref[...], (8, LANES))
    drift_x = jnp.broadcast_to(CURRENT_GAIN * jnp.tanh(f_in_ref[0:1, :]), (8, LANES))
    drift_y = jnp.broadcast_to(CURRENT_GAIN * jnp.tanh(f_in_ref[L : L + 1, :]), (8, LANES))

    def advect(m, carry):
        for n in range(16):
            rows = tile_rows(m * 128 + n * 8)
            tile = e_in_ref[rows, :]
            speed = speed_ref[rows, :]
            a_x = speed[:, 0:1] + drift_x
            a_y = speed[:, 1:2] + drift_y
            west, east, south, north = neighbours(tile, n, m, *halos)
            moved = (
                tile
                - jnp.maximum(a_x, 0.0) * (tile - west)
                - jnp.minimum(a_x, 0.0) * (east - tile)
                - jnp.maximum(a_y, 0.0) * (tile - south)
                - jnp.minimum(a_y, 0.0) * (north - tile)
            )
            e_ref[rows, :] = moved * wet
        return carry

    lax.fori_loop(0, channels // 128, advect, 0)

    sub = lax.broadcasted_iota(jnp.int32, (8, LANES), 0)
    here = [sub == s for s in range(8)]

    def gathered(base):
        picked = []
        for j in range(4):
            rows = None
            for s in range(8):
                row = e_ref[pl.ds(index_ref[base + j * 8 + s], 8, stride=0), :]
                rows = row if rows is None else jnp.where(here[s], row, rows)
            picked.append(rows)
        first, second, third, fourth = picked
        return first * second * (third + fourth) - third * fourth * (first + second)

    def interactions(i, carry):
        for t in range(2):
            base = i * 128 + t * 64
            both = jnp.concatenate([gathered(base), gathered(base + 32)], axis=0)
            inter_ref[pl.ds(pl.multiple_of(i * 32 + t * 16, 16), 16), :] = both.astype(jnp.bfloat16)
        return carry

    def substep(_, carry):
        lax.fori_loop(0, quads // 32, interactions, 0)
        growth = jnp.dot(coupling_ref[...], inter_ref[...], preferred_element_type=jnp.float32)
        gained = SOURCE_GAIN * growth / (1.0 + SOURCE_GAIN * jnp.abs(growth))
        e_ref[0:channels, :] = e_ref[0:channels, :] + wet_ref[...] * gained
        return carry

    lax.fori_loop(0, SUB, substep, 0)

    energy = e_ref[0:channels, :]
    e_out_ref[...] = energy
    stokes = jnp.dot(
        profile_ref[...], energy, precision=lax.Precision.HIGHEST, preferred_element_type=jnp.float32
    )

    tiles = [f_in_ref[n * 8 : n * 8 + 8, :] for n in range(FIELDS // 8)]
    around = [neighbours(tile, n, channels // 128, *halos) for n, tile in enumerate(tiles)]
    half = L // 8
    level = lax.broadcasted_iota(jnp.int32, (L, LANES), 0)

    def field(lo):
        whole = jnp.concatenate(tiles[lo : lo + half], axis=0)
        sides = [jnp.concatenate([around[n][d] for n in range(lo, lo + half)], axis=0) for d in range(4)]
        above = jnp.where(level == 0, 0.0, roll(whole, 1, 0))
        below = jnp.where(level == L - 1, 0.0, roll(whole, -1, 0))
        mixed = VISCOSITY * (sides[1] + sides[0] + sides[3] + sides[2] - 4.0 * whole) + MIXING * (
            below + above - 2.0 * whole
        )
        return whole, sides, mixed

    flow_x, sides_x, mixed_x = field(0)
    flow_y, sides_y, mixed_y = field(half)
    vortex = 0.5 * (sides_y[1] - sides_y[0]) - 0.5 * (sides_x[3] - sides_x[2])
    stokes_x = stokes[0:L]
    stokes_y = stokes[L : 2 * L]
    f_out_ref[0:L, :] = flow_x + CORIOLIS * (flow_y + stokes_y) + vortex * stokes_y + mixed_x
    f_out_ref[L : 2 * L, :] = flow_y - CORIOLIS * (flow_x + stokes_x) - vortex * stokes_x + mixed_y

    if not last:
        pack_all(e_ref, f_out_ref, channels, edges)


def exchange(values, axis):
    rows, lanes = values.shape
    moved = lax.all_to_all(values.reshape(rows, 1, lanes), axis, split_axis=0, concat_axis=0, tiled=True)
    return moved.reshape(rows, lanes)


def send_edges(edges):
    up, down, east, west = edges

    def shift(value, axis, by):
        count = lax.axis_size(axis)
        pairs = [(i, i + by) for i in range(count) if 0 <= i + by < count]
        return lax.ppermute(value, axis, pairs)

    south = shift(up, "grp", 1)
    north = shift(down, "grp", -1)
    from_west = shift(east, "comp", 1)
    from_east = shift(west, "comp", -1)
    return south, north, from_west, from_east


def local(spectrum, group_speed, sea_mask, quad_index, coupling, stokes_kernel, ocean_flow):
    parts, rows_local, columns = spectrum.shape
    cols_local = ocean_flow.shape[3]
    peers = columns // cols_local
    groups = ocean_flow.shape[2] // rows_local
    channels = parts * peers
    quads = quad_index.shape[1]
    comp_place = lax.axis_index("comp")
    group_place = lax.axis_index("grp")

    float_of = lambda *shape: jax.ShapeDtypeStruct(shape, jnp.float32)
    edge_shapes = [float_of((channels // 64 + 1) * 8, LANES)] * 2 + [
        float_of((channels // 128 + 1) * 8, LANES)
    ] * 2

    wet_rows = (sea_mask == 1).astype(jnp.float32)
    wet = lax.dynamic_slice_in_dim(wet_rows, comp_place * cols_local, cols_local, 1).reshape(1, LANES)
    flow = lax.dynamic_slice_in_dim(ocean_flow, group_place * rows_local, rows_local, 2).reshape(FIELDS, LANES)
    index = quad_index.reshape(4, quads // 8, 8).transpose(1, 0, 2).reshape(4 * quads)
    speed = group_speed.T

    sent = pl.pallas_call(
        to_points_kernel, out_shape=float_of(channels, LANES), in_specs=[VMEM], out_specs=VMEM, compiler_params=SMALL, name="to_points"
    )(spectrum)
    energy = exchange(sent, "comp")
    edges = pl.pallas_call(
        edges_kernel, out_shape=edge_shapes, in_specs=[VMEM] * 2, out_specs=[VMEM] * 4, compiler_params=SMALL, name="edges"
    )(energy, flow)
    for iteration in range(STEPS):
        last = iteration == STEPS - 1
        halos = send_edges(edges)
        outs = [float_of(channels, LANES), float_of(FIELDS, LANES)] + ([] if last else edge_shapes)
        energy, flow, *edges = pl.pallas_call(
            functools.partial(step_kernel, last),
            out_shape=outs,
            in_specs=[SMEM] + [VMEM] * 10,
            out_specs=[VMEM] * len(outs),
            scratch_shapes=[pltpu.VMEM((channels + 8, LANES), jnp.float32), pltpu.VMEM((quads, LANES), jnp.bfloat16)],
            compiler_params=SMALL,
            name="last_step" if last else "step",
        )(index, energy, flow, wet, speed, coupling, stokes_kernel, *halos)
    returned = exchange(energy, "comp")
    forecast = pl.pallas_call(
        from_points_kernel,
        out_shape=float_of(parts, rows_local, columns),
        in_specs=[VMEM],
        out_specs=VMEM,
        compiler_params=SMALL,
        name="from_points",
    )(returned)
    copies = jnp.broadcast_to(flow[None], (groups, FIELDS, LANES)).reshape(groups * FIELDS, LANES)
    rows = exchange(copies, "grp").reshape(groups, 2, L, rows_local, cols_local)
    ocean = rows.transpose(1, 2, 0, 3, 4).reshape(2, L, groups * rows_local, cols_local)
    return forecast, ocean


def solution(mesh):
    in_specs = (
        P("comp", "grp", None),
        P(),
        P("grp", None),
        P(),
        P(),
        P(),
        P(None, None, None, "comp"),
    )
    out_specs = (P("comp", "grp", None), P(None, None, None, "comp"))
    return jax.shard_map(local, mesh=mesh, in_specs=in_specs, out_specs=out_specs, check_vma=False)
```

```python
import functools

import jax
import jax.numpy as jnp
from jax import lax
from jax.experimental import pallas as pl
from jax.experimental.pallas import tpu as pltpu
from jax.sharding import PartitionSpec as P

L = 16
STEPS = 2
SUB = 3

SOURCE_GAIN = 0.3
CURRENT_GAIN = 0.25
CORIOLIS = 0.3
VISCOSITY = 0.15
MIXING = 0.15

ROWS = 8
COLS = 16
LANES = 128
FIELDS = 2 * L

VMEM = pl.BlockSpec(memory_space=pltpu.VMEM)
SMEM = pl.BlockSpec(memory_space=pltpu.SMEM)
SMALL = pltpu.CompilerParams(vmem_limit_bytes=16 * 2**20)


def roll(x, shift, axis=1):
    shift %= x.shape[axis]
    return pltpu.roll(x, shift, axis) if shift else x


def lane_places():
    lane = lax.broadcasted_iota(jnp.int32, (8, LANES), 1)
    return lane // COLS, lane % COLS


def exchange_blocks(x):
    sub = lax.broadcasted_iota(jnp.int32, (8, LANES), 0)
    block, _ = lane_places()
    for bit in (1, 2, 4):
        in_sub = (sub & bit) != 0
        in_block = (block & bit) != 0
        up = roll(roll(x, -bit, 0), bit * COLS)
        down = roll(roll(x, bit, 0), -bit * COLS)
        x = jnp.where(in_sub == in_block, x, jnp.where(in_block, up, down))
    return x


def to_points_kernel(x_ref, o_ref):
    parts = x_ref.shape[0]

    def one(k, carry):
        for j in range(x_ref.shape[2] // LANES):
            tile = exchange_blocks(x_ref[k, :, j * LANES : (j + 1) * LANES])
            o_ref[pl.ds(j * 8 * parts + k, 8, stride=parts), :] = tile
        return carry

    lax.fori_loop(0, parts, one, 0, unroll=3)


def from_points_kernel(x_ref, o_ref):
    parts = o_ref.shape[0]

    def one(k, carry):
        for j in range(o_ref.shape[2] // LANES):
            tile = x_ref[pl.ds(j * 8 * parts + k, 8, stride=parts), :]
            o_ref[k, :, j * LANES : (j + 1) * LANES] = exchange_blocks(tile)
        return carry

    lax.fori_loop(0, parts, one, 0, unroll=3)


def tile_rows(start, count=8):
    return pl.ds(start if isinstance(start, int) else pl.multiple_of(start, 8), count)


def pack_group(load, count, m, up_ref, down_ref, east_ref, west_ref):
    block, col = lane_places()
    east = west = None
    for h in range((count + 7) // 8):
        up = down = None
        for i in range(min(8, count - 8 * h)):
            n = 8 * h + i
            tile = load(n)
            u = roll(tile, (i - (ROWS - 1)) * COLS)
            d = roll(tile, i * COLS)
            e = roll(tile, n - (COLS - 1))
            w = roll(tile, n)
            up = u if up is None else jnp.where(block == i, u, up)
            down = d if down is None else jnp.where(block == i, d, down)
            east = e if east is None else jnp.where(col == n, e, east)
            west = w if west is None else jnp.where(col == n, w, west)
        up_ref[tile_rows((2 * m + h) * 8), :] = up
        down_ref[tile_rows((2 * m + h) * 8), :] = down
    east_ref[tile_rows(m * 8), :] = east
    west_ref[tile_rows(m * 8), :] = west


def pack_all(e_ref, f_ref, channels, edges):
    def one(m, carry):
        pack_group(lambda n: e_ref[tile_rows(m * 128 + n * 8), :], 16, m, *edges)
        return carry

    lax.fori_loop(0, channels // 128, one, 0)
    pack_group(lambda n: f_ref[n * 8 : n * 8 + 8, :], FIELDS // 8, channels // 128, *edges)


def neighbours(tile, n, m, south_ref, north_ref, west_ref, east_ref):
    block, col = lane_places()
    h, i = divmod(n, 8)
    south = roll(south_ref[tile_rows((2 * m + h) * 8), :], -i * COLS)
    north = roll(north_ref[tile_rows((2 * m + h) * 8), :], (ROWS - 1 - i) * COLS)
    west = roll(west_ref[tile_rows(m * 8), :], -n)
    east = roll(east_ref[tile_rows(m * 8), :], COLS - 1 - n)
    return (
        jnp.where(col == 0, west, roll(tile, 1)),
        jnp.where(col == COLS - 1, east, roll(tile, -1)),
        jnp.where(block == 0, south, roll(tile, COLS)),
        jnp.where(block == ROWS - 1, north, roll(tile, -COLS)),
    )


def edges_kernel(e_ref, f_ref, *edges):
    pack_all(e_ref, f_ref, e_ref.shape[0], edges)


def step_kernel(
    last,
    index_ref,
    e_in_ref,
    f_in_ref,
    wet_ref,
    speed_ref,
    coupling_ref,
    profile_ref,
    south_ref,
    north_ref,
    west_ref,
    east_ref,
    e_out_ref,
    f_out_ref,
    *rest,
):
    edges, (e_ref, inter_ref) = rest[:-2], rest[-2:]
    channels = e_in_ref.shape[0]
    quads = inter_ref.shape[0]
    halos = (south_ref, north_ref, west_ref, east_ref)
    wet = jnp.broadcast_to(wet_ref[...], (8, LANES))
    drift_x = jnp.broadcast_to(CURRENT_GAIN * jnp.tanh(f_in_ref[0:1, :]), (8, LANES))
    drift_y = jnp.broadcast_to(CURRENT_GAIN * jnp.tanh(f_in_ref[L : L + 1, :]), (8, LANES))

    def advect(m, carry):
        group = pl.ds(pl.multiple_of(m * 128, 128), 128)
        speed_x = jnp.broadcast_to(speed_ref[0:1, group], (128, LANES)).T
        speed_y = jnp.broadcast_to(speed_ref[1:2, group], (128, LANES)).T
        for n in range(16):
            rows = tile_rows(m * 128 + n * 8)
            tile = e_in_ref[rows, :]
            a_x = speed_x[n * 8 : n * 8 + 8] + drift_x
            a_y = speed_y[n * 8 : n * 8 + 8] + drift_y
            west, east, south, north = neighbours(tile, n, m, *halos)
            moved = (
                tile
                - jnp.maximum(a_x, 0.0) * (tile - west)
                - jnp.minimum(a_x, 0.0) * (east - tile)
                - jnp.maximum(a_y, 0.0) * (tile - south)
                - jnp.minimum(a_y, 0.0) * (north - tile)
            )
            e_ref[rows, :] = moved * wet
        return carry

    lax.fori_loop(0, channels // 128, advect, 0)

    sub = lax.broadcasted_iota(jnp.int32, (8, LANES), 0)
    here = [sub == s for s in range(8)]

    def gathered(quad):
        picked = []
        for j in range(4):
            rows = None
            for s in range(8):
                row = e_ref[pl.ds(index_ref[j, quad + s], 8, stride=0), :]
                rows = row if rows is None else jnp.where(here[s], row, rows)
            picked.append(rows)
        first, second, third, fourth = picked
        return first * second * (third + fourth) - third * fourth * (first + second)

    def substep(_, carry):
        for quad in range(0, quads, 16):
            both = jnp.concatenate([gathered(quad), gathered(quad + 8)], axis=0)
            inter_ref[quad : quad + 16, :] = both.astype(jnp.bfloat16)
        growth = jnp.dot(coupling_ref[...], inter_ref[...], preferred_element_type=jnp.float32)
        gained = SOURCE_GAIN * growth / (1.0 + SOURCE_GAIN * jnp.abs(growth))
        e_ref[0:channels, :] = e_ref[0:channels, :] + wet_ref[...] * gained
        return carry

    lax.fori_loop(0, SUB, substep, 0)

    energy = e_ref[0:channels, :]
    e_out_ref[...] = energy
    stokes = jnp.dot(
        profile_ref[...], energy, precision=lax.Precision.HIGHEST, preferred_element_type=jnp.float32
    )

    tiles = [f_in_ref[n * 8 : n * 8 + 8, :] for n in range(FIELDS // 8)]
    around = [neighbours(tile, n, channels // 128, *halos) for n, tile in enumerate(tiles)]
    half = L // 8
    level = lax.broadcasted_iota(jnp.int32, (L, LANES), 0)

    def field(lo):
        whole = jnp.concatenate(tiles[lo : lo + half], axis=0)
        sides = [jnp.concatenate([around[n][d] for n in range(lo, lo + half)], axis=0) for d in range(4)]
        above = jnp.where(level == 0, 0.0, roll(whole, 1, 0))
        below = jnp.where(level == L - 1, 0.0, roll(whole, -1, 0))
        mixed = VISCOSITY * (sides[1] + sides[0] + sides[3] + sides[2] - 4.0 * whole) + MIXING * (
            below + above - 2.0 * whole
        )
        return whole, sides, mixed

    flow_x, sides_x, mixed_x = field(0)
    flow_y, sides_y, mixed_y = field(half)
    vortex = 0.5 * (sides_y[1] - sides_y[0]) - 0.5 * (sides_x[3] - sides_x[2])
    stokes_x = stokes[0:L]
    stokes_y = stokes[L : 2 * L]
    f_out_ref[0:L, :] = flow_x + CORIOLIS * (flow_y + stokes_y) + vortex * stokes_y + mixed_x
    f_out_ref[L : 2 * L, :] = flow_y - CORIOLIS * (flow_x + stokes_x) - vortex * stokes_x + mixed_y

    if not last:
        pack_all(e_ref, f_out_ref, channels, edges)


def exchange(values, axis):
    peers = lax.axis_size(axis)
    lines = values.reshape(peers, 1, values.size // peers)
    moved = lax.all_to_all(lines, axis, split_axis=0, concat_axis=0, tiled=True)
    return moved.reshape(values.shape)


def gather_tiles(flow, groups, group_place):
    held = flow[None]
    bit = groups // 2
    while bit:
        other = lax.ppermute(held, "grp", [(i, i ^ bit) for i in range(groups)])
        upper = (group_place & bit) != 0
        held = jnp.concatenate([jnp.where(upper, other, held), jnp.where(upper, held, other)], axis=0)
        bit //= 2
    return held


def send_edges(edges):
    up, down, east, west = edges

    def shift(value, axis, by):
        count = lax.axis_size(axis)
        pairs = [(i, i + by) for i in range(count) if 0 <= i + by < count]
        return lax.ppermute(value, axis, pairs)

    south = shift(up, "grp", 1)
    north = shift(down, "grp", -1)
    from_west = shift(east, "comp", 1)
    from_east = shift(west, "comp", -1)
    return south, north, from_west, from_east


def local(spectrum, group_speed, sea_mask, quad_index, coupling, stokes_kernel, ocean_flow):
    parts, rows_local, columns = spectrum.shape
    cols_local = ocean_flow.shape[3]
    peers = columns // cols_local
    groups = ocean_flow.shape[2] // rows_local
    channels = parts * peers
    quads = quad_index.shape[1]
    comp_place = lax.axis_index("comp")
    group_place = lax.axis_index("grp")

    float_of = lambda *shape: jax.ShapeDtypeStruct(shape, jnp.float32)
    edge_shapes = [float_of((channels // 64 + 1) * 8, LANES)] * 2 + [
        float_of((channels // 128 + 1) * 8, LANES)
    ] * 2

    wet_rows = (sea_mask == 1).astype(jnp.float32)
    wet = lax.dynamic_slice_in_dim(wet_rows, comp_place * cols_local, cols_local, 1).reshape(1, LANES)
    flow = lax.dynamic_slice_in_dim(ocean_flow, group_place * rows_local, rows_local, 2).reshape(FIELDS, LANES)

    sent = pl.pallas_call(
        to_points_kernel, out_shape=float_of(channels, LANES), in_specs=[VMEM], out_specs=VMEM, compiler_params=SMALL, name="to_points"
    )(spectrum)
    energy, wet, flow = lax.optimization_barrier((exchange(sent, "comp"), wet, flow))
    edges = pl.pallas_call(
        edges_kernel, out_shape=edge_shapes, in_specs=[VMEM] * 2, out_specs=[VMEM] * 4, compiler_params=SMALL, name="edges"
    )(energy, flow)
    for iteration in range(STEPS):
        last = iteration == STEPS - 1
        halos = send_edges(edges)
        outs = [float_of(channels, LANES), float_of(FIELDS, LANES)] + ([] if last else edge_shapes)
        energy, flow, *edges = pl.pallas_call(
            functools.partial(step_kernel, last),
            out_shape=outs,
            in_specs=[SMEM] + [VMEM] * 10,
            out_specs=[VMEM] * len(outs),
            scratch_shapes=[pltpu.VMEM((channels + 8, LANES), jnp.float32), pltpu.VMEM((quads, LANES), jnp.bfloat16)],
            compiler_params=SMALL,
            name="last_step" if last else "step",
        )(quad_index, energy, flow, wet, group_speed, coupling, stokes_kernel, *halos)
    returned = exchange(energy, "comp")
    forecast = pl.pallas_call(
        from_points_kernel,
        out_shape=float_of(parts, rows_local, columns),
        in_specs=[VMEM],
        out_specs=VMEM,
        compiler_params=SMALL,
        name="from_points",
    )(returned)
    bits = groups.bit_length() - 1
    tiles = gather_tiles(flow, groups, group_place).reshape((2,) * bits + (2, L, rows_local, cols_local))
    order = (bits, bits + 1) + tuple(range(bits - 1, -1, -1)) + (bits + 2, bits + 3)
    ocean = tiles.transpose(order).reshape(2, L, groups * rows_local, cols_local)
    return forecast, ocean


def solution(mesh):
    in_specs = (
        P("comp", "grp", None),
        P(),
        P("grp", None),
        P(),
        P(),
        P(),
        P(None, None, None, "comp"),
    )
    out_specs = (P("comp", "grp", None), P(None, None, None, "comp"))
    return jax.shard_map(local, mesh=mesh, in_specs=in_specs, out_specs=out_specs, check_vma=False)
```

```python
import functools

import jax
import jax.numpy as jnp
from jax import lax
from jax.experimental import pallas as pl
from jax.experimental.pallas import tpu as pltpu
from jax.sharding import PartitionSpec as P

L = 16
STEPS = 2
SUB = 3

SOURCE_GAIN = 0.3
CURRENT_GAIN = 0.25
CORIOLIS = 0.3
VISCOSITY = 0.15
MIXING = 0.15

ROWS = 8
COLS = 16
LANES = 128
FIELDS = 2 * L

VMEM = pl.BlockSpec(memory_space=pltpu.VMEM)
SMEM = pl.BlockSpec(memory_space=pltpu.SMEM)
SMALL = pltpu.CompilerParams(vmem_limit_bytes=16 * 2**20)


def roll(x, shift, axis=1):
    shift %= x.shape[axis]
    return pltpu.roll(x, shift, axis) if shift else x


def lane_places():
    lane = lax.broadcasted_iota(jnp.int32, (8, LANES), 1)
    return lane // COLS, lane % COLS


def exchange_blocks(x):
    sub = lax.broadcasted_iota(jnp.int32, (8, LANES), 0)
    block, _ = lane_places()
    for bit in (1, 2, 4):
        in_sub = (sub & bit) != 0
        in_block = (block & bit) != 0
        up = roll(roll(x, -bit, 0), bit * COLS)
        down = roll(roll(x, bit, 0), -bit * COLS)
        x = jnp.where(in_sub == in_block, x, jnp.where(in_block, up, down))
    return x


def to_points_kernel(x_ref, o_ref):
    parts = x_ref.shape[0]

    def one(k, carry):
        for j in range(x_ref.shape[2] // LANES):
            tile = exchange_blocks(x_ref[k, :, j * LANES : (j + 1) * LANES])
            o_ref[pl.ds(j * 8 * parts + k, 8, stride=parts), :] = tile
        return carry

    lax.fori_loop(0, parts, one, 0, unroll=3)


def from_points_kernel(x_ref, o_ref):
    parts = o_ref.shape[0]

    def one(k, carry):
        for j in range(o_ref.shape[2] // LANES):
            tile = x_ref[pl.ds(j * 8 * parts + k, 8, stride=parts), :]
            o_ref[k, :, j * LANES : (j + 1) * LANES] = exchange_blocks(tile)
        return carry

    lax.fori_loop(0, parts, one, 0, unroll=3)


def tile_rows(start, count=8):
    return pl.ds(start if isinstance(start, int) else pl.multiple_of(start, 8), count)


def pack_group(load, count, m, odd_ref, rows_a_ref, rows_b_ref, cols_a_ref, cols_b_ref):
    odd_row = odd_ref[0] == 1
    odd_col = odd_ref[1] == 1
    block, col = lane_places()
    east = west = None
    for h in range((count + 7) // 8):
        up = down = None
        for i in range(min(8, count - 8 * h)):
            n = 8 * h + i
            tile = load(n)
            u = roll(tile, (i - (ROWS - 1)) * COLS)
            d = roll(tile, i * COLS)
            e = roll(tile, n - (COLS - 1))
            w = roll(tile, n)
            up = u if up is None else jnp.where(block == i, u, up)
            down = d if down is None else jnp.where(block == i, d, down)
            east = e if east is None else jnp.where(col == n, e, east)
            west = w if west is None else jnp.where(col == n, w, west)
        rows_a_ref[tile_rows((2 * m + h) * 8), :] = jnp.where(odd_row, down, up)
        rows_b_ref[tile_rows((2 * m + h) * 8), :] = jnp.where(odd_row, up, down)
    cols_a_ref[tile_rows(m * 8), :] = jnp.where(odd_col, west, east)
    cols_b_ref[tile_rows(m * 8), :] = jnp.where(odd_col, east, west)


def pack_all(e_ref, f_ref, channels, odd_ref, edges):
    def one(m, carry):
        pack_group(lambda n: e_ref[tile_rows(m * 128 + n * 8), :], 16, m, odd_ref, *edges)
        return carry

    lax.fori_loop(0, channels // 128, one, 0)
    pack_group(lambda n: f_ref[n * 8 : n * 8 + 8, :], FIELDS // 8, channels // 128, odd_ref, *edges)


def neighbours(tile, n, m, south_ref, north_ref, west_ref, east_ref):
    block, col = lane_places()
    h, i = divmod(n, 8)
    south = roll(south_ref[tile_rows((2 * m + h) * 8), :], -i * COLS)
    north = roll(north_ref[tile_rows((2 * m + h) * 8), :], (ROWS - 1 - i) * COLS)
    west = roll(west_ref[tile_rows(m * 8), :], -n)
    east = roll(east_ref[tile_rows(m * 8), :], COLS - 1 - n)
    return (
        jnp.where(col == 0, west, roll(tile, 1)),
        jnp.where(col == COLS - 1, east, roll(tile, -1)),
        jnp.where(block == 0, south, roll(tile, COLS)),
        jnp.where(block == ROWS - 1, north, roll(tile, -COLS)),
    )


def edges_kernel(odd_ref, e_ref, f_ref, *edges):
    pack_all(e_ref, f_ref, e_ref.shape[0], odd_ref, edges)


def step_kernel(
    last,
    odd_ref,
    index_ref,
    e_in_ref,
    f_in_ref,
    wet_ref,
    speed_ref,
    coupling_ref,
    profile_ref,
    rows_a_ref,
    rows_b_ref,
    cols_a_ref,
    cols_b_ref,
    e_out_ref,
    f_out_ref,
    *rest,
):
    edges, (e_ref, inter_ref, *halos) = rest[:-6], rest[-6:]
    channels = e_in_ref.shape[0]
    quads = inter_ref.shape[0]
    odd_row = odd_ref[0] == 1
    odd_col = odd_ref[1] == 1
    south_ref, north_ref, west_ref, east_ref = halos
    south_ref[...] = jnp.where(odd_row, rows_a_ref[...], rows_b_ref[...])
    north_ref[...] = jnp.where(odd_row, rows_b_ref[...], rows_a_ref[...])
    west_ref[...] = jnp.where(odd_col, cols_a_ref[...], cols_b_ref[...])
    east_ref[...] = jnp.where(odd_col, cols_b_ref[...], cols_a_ref[...])
    wet = jnp.broadcast_to(wet_ref[...], (8, LANES))
    drift_x = jnp.broadcast_to(CURRENT_GAIN * jnp.tanh(f_in_ref[0:1, :]), (8, LANES))
    drift_y = jnp.broadcast_to(CURRENT_GAIN * jnp.tanh(f_in_ref[L : L + 1, :]), (8, LANES))

    def advect(m, carry):
        group = pl.ds(pl.multiple_of(m * 128, 128), 128)
        speed_x = jnp.broadcast_to(speed_ref[0:1, group], (128, LANES)).T
        speed_y = jnp.broadcast_to(speed_ref[1:2, group], (128, LANES)).T
        for n in range(16):
            rows = tile_rows(m * 128 + n * 8)
            tile = e_in_ref[rows, :]
            a_x = speed_x[n * 8 : n * 8 + 8] + drift_x
            a_y = speed_y[n * 8 : n * 8 + 8] + drift_y
            west, east, south, north = neighbours(tile, n, m, *halos)
            moved = (
                tile
                - jnp.maximum(a_x, 0.0) * (tile - west)
                - jnp.minimum(a_x, 0.0) * (east - tile)
                - jnp.maximum(a_y, 0.0) * (tile - south)
                - jnp.minimum(a_y, 0.0) * (north - tile)
            )
            e_ref[rows, :] = moved * wet
        return carry

    lax.fori_loop(0, channels // 128, advect, 0)

    sub = lax.broadcasted_iota(jnp.int32, (8, LANES), 0)
    here = [sub == s for s in range(8)]

    def gathered(quad):
        picked = []
        for j in range(4):
            rows = None
            for s in range(8):
                row = e_ref[pl.ds(index_ref[j, quad + s], 8, stride=0), :]
                rows = row if rows is None else jnp.where(here[s], row, rows)
            picked.append(rows)
        first, second, third, fourth = picked
        return first * second * (third + fourth) - third * fourth * (first + second)

    def substep(_, carry):
        for quad in range(0, quads, 16):
            both = jnp.concatenate([gathered(quad), gathered(quad + 8)], axis=0)
            inter_ref[quad : quad + 16, :] = both.astype(jnp.bfloat16)
        growth = jnp.dot(coupling_ref[...], inter_ref[...], preferred_element_type=jnp.float32)
        gained = SOURCE_GAIN * growth / (1.0 + SOURCE_GAIN * jnp.abs(growth))
        e_ref[0:channels, :] = e_ref[0:channels, :] + wet_ref[...] * gained
        return carry

    lax.fori_loop(0, SUB, substep, 0)

    energy = e_ref[0:channels, :]
    e_out_ref[...] = energy
    stokes = jnp.dot(
        profile_ref[...], energy, precision=lax.Precision.HIGHEST, preferred_element_type=jnp.float32
    )

    tiles = [f_in_ref[n * 8 : n * 8 + 8, :] for n in range(FIELDS // 8)]
    around = [neighbours(tile, n, channels // 128, *halos) for n, tile in enumerate(tiles)]
    half = L // 8
    level = lax.broadcasted_iota(jnp.int32, (L, LANES), 0)

    def field(lo):
        whole = jnp.concatenate(tiles[lo : lo + half], axis=0)
        sides = [jnp.concatenate([around[n][d] for n in range(lo, lo + half)], axis=0) for d in range(4)]
        above = jnp.where(level == 0, 0.0, roll(whole, 1, 0))
        below = jnp.where(level == L - 1, 0.0, roll(whole, -1, 0))
        mixed = VISCOSITY * (sides[1] + sides[0] + sides[3] + sides[2] - 4.0 * whole) + MIXING * (
            below + above - 2.0 * whole
        )
        return whole, sides, mixed

    flow_x, sides_x, mixed_x = field(0)
    flow_y, sides_y, mixed_y = field(half)
    vortex = 0.5 * (sides_y[1] - sides_y[0]) - 0.5 * (sides_x[3] - sides_x[2])
    stokes_x = stokes[0:L]
    stokes_y = stokes[L : 2 * L]
    f_out_ref[0:L, :] = flow_x + CORIOLIS * (flow_y + stokes_y) + vortex * stokes_y + mixed_x
    f_out_ref[L : 2 * L, :] = flow_y - CORIOLIS * (flow_x + stokes_x) - vortex * stokes_x + mixed_y

    if not last:
        pack_all(e_ref, f_out_ref, channels, odd_ref, edges)


def exchange(values, axis):
    peers = lax.axis_size(axis)
    lines = values.reshape(peers, 1, values.size // peers)
    moved = lax.all_to_all(lines, axis, split_axis=0, concat_axis=0, tiled=True)
    return moved.reshape(values.shape)


def swap_edges(edges):
    rows_a, rows_b, cols_a, cols_b = edges

    def swap(value, axis, shift):
        count = lax.axis_size(axis)
        partner = [((i + shift) ^ 1) - shift for i in range(count)]
        return lax.ppermute(value, axis, [(i, j) for i, j in enumerate(partner) if 0 <= j < count])

    from_b = swap(rows_b, "grp", 1)
    from_a = swap(rows_a, "grp", 0)
    return (from_a, from_b, swap(cols_b, "comp", 1), swap(cols_a, "comp", 0))


def ordered(upper, mine, other):
    return jnp.where(upper, other, mine), jnp.where(upper, mine, other)


def local(spectrum, group_speed, sea_mask, quad_index, coupling, stokes_kernel, ocean_flow):
    parts, rows_local, columns = spectrum.shape
    cols_local = ocean_flow.shape[3]
    peers = columns // cols_local
    groups = ocean_flow.shape[2] // rows_local
    channels = parts * peers
    quads = quad_index.shape[1]
    comp_place = lax.axis_index("comp")
    group_place = lax.axis_index("grp")

    float_of = lambda *shape: jax.ShapeDtypeStruct(shape, jnp.float32)
    edge_shapes = [float_of((channels // 64 + 1) * 8, LANES)] * 2 + [
        float_of((channels // 128 + 1) * 8, LANES)
    ] * 2

    wet_rows = (sea_mask == 1).astype(jnp.float32)
    wet = lax.dynamic_slice_in_dim(wet_rows, comp_place * cols_local, cols_local, 1).reshape(1, LANES)
    flow = lax.dynamic_slice_in_dim(ocean_flow, group_place * rows_local, rows_local, 2).reshape(FIELDS, LANES)

    odd = jnp.stack([group_place & 1, comp_place & 1]).astype(jnp.int32)

    sent = pl.pallas_call(
        to_points_kernel, out_shape=float_of(channels, LANES), in_specs=[VMEM], out_specs=VMEM, compiler_params=SMALL, name="to_points"
    )(spectrum)
    energy, wet, flow, odd = lax.optimization_barrier((exchange(sent, "comp"), wet, flow, odd))
    edges = pl.pallas_call(
        edges_kernel, out_shape=edge_shapes, in_specs=[SMEM, VMEM, VMEM], out_specs=[VMEM] * 4, compiler_params=SMALL, name="edges"
    )(odd, energy, flow)
    for iteration in range(STEPS):
        last = iteration == STEPS - 1
        from_a, from_b, from_cols_b, from_cols_a = swap_edges(edges)
        outs = [float_of(channels, LANES), float_of(FIELDS, LANES)] + ([] if last else edge_shapes)
        energy, flow, *edges = pl.pallas_call(
            functools.partial(step_kernel, last),
            out_shape=outs,
            in_specs=[SMEM] * 2 + [VMEM] * 10,
            out_specs=[VMEM] * len(outs),
            scratch_shapes=[pltpu.VMEM((channels + 8, LANES), jnp.float32), pltpu.VMEM((quads, LANES), jnp.bfloat16)]
            + [pltpu.VMEM(edge.shape, jnp.float32) for edge in edge_shapes],
            compiler_params=SMALL,
            name="last_step" if last else "step",
        )(odd, quad_index, energy, flow, wet, group_speed, coupling, stokes_kernel, from_a, from_b, from_cols_a, from_cols_b)
    returned = exchange(energy, "comp")
    half = groups // 2
    far = lax.ppermute(flow, "grp", [(i, i ^ half) for i in range(groups)])
    held = jnp.stack(ordered((group_place & half) != 0, flow, far))
    held, returned = lax.optimization_barrier((held, returned))
    tiles = [held] + [lax.ppermute(held, "grp", [(i, i ^ by) for i in range(groups)]) for by in range(1, half)]
    forecast = pl.pallas_call(
        from_points_kernel,
        out_shape=float_of(parts, rows_local, columns),
        in_specs=[VMEM],
        out_specs=VMEM,
        compiler_params=SMALL,
        name="from_points",
    )(returned)
    bit = 1
    while bit < half:
        upper = (group_place & bit) != 0
        tiles = [jnp.where(upper, tiles[j ^ bit], tiles[j]) for j in range(half)]
        bit *= 2
    fields = jnp.stack(tiles).reshape(half, 2, 2, L, rows_local, cols_local)
    ocean = fields.transpose(2, 3, 1, 0, 4, 5).reshape(2, L, groups * rows_local, cols_local)
    return forecast, ocean


def solution(mesh):
    in_specs = (
        P("comp", "grp", None),
        P(),
        P("grp", None),
        P(),
        P(),
        P(),
        P(None, None, None, "comp"),
    )
    out_specs = (P("comp", "grp", None), P(None, None, None, "comp"))
    return jax.shard_map(local, mesh=mesh, in_specs=in_specs, out_specs=out_specs, check_vma=False)
```

```python
import functools

import jax
import jax.numpy as jnp
from jax import lax
from jax.experimental import pallas as pl
from jax.experimental.pallas import tpu as pltpu
from jax.sharding import PartitionSpec as P

L = 16
STEPS = 2
SUB = 3

SOURCE_GAIN = 0.3
CURRENT_GAIN = 0.25
CORIOLIS = 0.3
VISCOSITY = 0.15
MIXING = 0.15

ROWS = 8
COLS = 16
LANES = 128
FIELDS = 2 * L

VMEM = pl.BlockSpec(memory_space=pltpu.VMEM)
SMEM = pl.BlockSpec(memory_space=pltpu.SMEM)
HBM = pl.BlockSpec(memory_space=pltpu.HBM)
STEP = pltpu.CompilerParams(vmem_limit_bytes=16 * 2**20)
SMALL = pltpu.CompilerParams(vmem_limit_bytes=16 * 2**20)


def roll(x, shift, axis=1):
    shift %= x.shape[axis]
    return pltpu.roll(x, shift, axis) if shift else x


def lane_places():
    lane = lax.broadcasted_iota(jnp.int32, (8, LANES), 1)
    return lane // COLS, lane % COLS


def exchange_blocks(x):
    sub = lax.broadcasted_iota(jnp.int32, (8, LANES), 0)
    block, _ = lane_places()
    for bit in (1, 2, 4):
        in_sub = (sub & bit) != 0
        in_block = (block & bit) != 0
        up = roll(roll(x, -bit, 0), bit * COLS)
        down = roll(roll(x, bit, 0), -bit * COLS)
        x = jnp.where(in_sub == in_block, x, jnp.where(in_block, up, down))
    return x


def to_points_kernel(x_hbm_ref, o_hbm_ref, x_ref, o_ref, in_sems, out_sems):
    parts = x_ref.shape[0]
    blocks = x_ref.shape[2] // LANES
    rows = 8 * parts

    def arriving(j):
        columns = pl.ds(j * LANES, LANES)
        return pltpu.make_async_copy(x_hbm_ref.at[:, :, columns], x_ref.at[:, :, columns], in_sems.at[j])

    def leaving(j):
        part = pl.ds(j * rows, rows)
        return pltpu.make_async_copy(o_ref.at[part, :], o_hbm_ref.at[part, :], out_sems.at[j])

    for j in range(blocks):
        arriving(j).start()
    for j in range(blocks):
        arriving(j).wait()

        def one(k, carry):
            tile = exchange_blocks(x_ref[k, :, j * LANES : (j + 1) * LANES])
            o_ref[pl.ds(j * rows + k, 8, stride=parts), :] = tile
            return carry

        lax.fori_loop(0, parts, one, 0, unroll=parts // 2)
        leaving(j).start()
    for j in range(blocks):
        leaving(j).wait()


def from_points_kernel(x_ref, o_hbm_ref, o_ref, out_sems):
    parts = o_ref.shape[0]
    blocks = o_ref.shape[2] // LANES

    def leaving(j):
        columns = pl.ds(j * LANES, LANES)
        return pltpu.make_async_copy(o_ref.at[:, :, columns], o_hbm_ref.at[:, :, columns], out_sems.at[j])

    for j in range(blocks):

        def one(k, carry):
            tile = x_ref[pl.ds(j * 8 * parts + k, 8, stride=parts), :]
            o_ref[k, :, j * LANES : (j + 1) * LANES] = exchange_blocks(tile)
            return carry

        lax.fori_loop(0, parts, one, 0, unroll=parts // 2)
        leaving(j).start()
    for j in range(blocks):
        leaving(j).wait()


def tile_rows(start, count=8):
    return pl.ds(start if isinstance(start, int) else pl.multiple_of(start, 8), count)


def parities():
    return lax.axis_index("grp") % 2 == 1, lax.axis_index("comp") % 2 == 1


def pack_group(load, count, m, rows_a_ref, rows_b_ref, cols_a_ref, cols_b_ref):
    odd_row, odd_col = parities()
    block, col = lane_places()
    east = west = None
    for h in range((count + 7) // 8):
        up = down = None
        for i in range(min(8, count - 8 * h)):
            n = 8 * h + i
            tile = load(n)
            u = roll(tile, (i - (ROWS - 1)) * COLS)
            d = roll(tile, i * COLS)
            e = roll(tile, n - (COLS - 1))
            w = roll(tile, n)
            up = u if up is None else jnp.where(block == i, u, up)
            down = d if down is None else jnp.where(block == i, d, down)
            east = e if east is None else jnp.where(col == n, e, east)
            west = w if west is None else jnp.where(col == n, w, west)
        rows_a_ref[tile_rows((2 * m + h) * 8), :] = jnp.where(odd_row, down, up)
        rows_b_ref[tile_rows((2 * m + h) * 8), :] = jnp.where(odd_row, up, down)
    cols_a_ref[tile_rows(m * 8), :] = jnp.where(odd_col, west, east)
    cols_b_ref[tile_rows(m * 8), :] = jnp.where(odd_col, east, west)


def pack_all(e_ref, f_ref, channels, edges):
    def one(m, carry):
        pack_group(lambda n: e_ref[tile_rows(m * 128 + n * 8), :], 16, m, *edges)
        return carry

    lax.fori_loop(0, channels // 128, one, 0)
    pack_group(lambda n: f_ref[n * 8 : n * 8 + 8, :], FIELDS // 8, channels // 128, *edges)


def neighbours(tile, n, m, south_ref, north_ref, west_ref, east_ref):
    block, col = lane_places()
    h, i = divmod(n, 8)
    south = roll(south_ref[tile_rows((2 * m + h) * 8), :], -i * COLS)
    north = roll(north_ref[tile_rows((2 * m + h) * 8), :], (ROWS - 1 - i) * COLS)
    west = roll(west_ref[tile_rows(m * 8), :], -n)
    east = roll(east_ref[tile_rows(m * 8), :], COLS - 1 - n)
    return (
        jnp.where(col == 0, west, roll(tile, 1)),
        jnp.where(col == COLS - 1, east, roll(tile, -1)),
        jnp.where(block == 0, south, roll(tile, COLS)),
        jnp.where(block == ROWS - 1, north, roll(tile, -COLS)),
    )


def edges_kernel(e_ref, f_ref, *edges):
    pack_all(e_ref, f_ref, e_ref.shape[0], edges)


def step_kernel(
    last,
    index_ref,
    e_in_ref,
    f_in_ref,
    vectors_ref,
    coupling_ref,
    rows_a_ref,
    rows_b_ref,
    cols_a_ref,
    cols_b_ref,
    e_out_ref,
    f_out_ref,
    *rest,
):
    edges, (e_ref, inter_ref, *halos) = rest[:-6], rest[-6:]
    channels = e_in_ref.shape[0]
    quads = inter_ref.shape[0]
    odd_row, odd_col = parities()
    south_ref, north_ref, west_ref, east_ref = halos
    south_ref[...] = jnp.where(odd_row, rows_a_ref[...], rows_b_ref[...])
    north_ref[...] = jnp.where(odd_row, rows_b_ref[...], rows_a_ref[...])
    west_ref[...] = jnp.where(odd_col, cols_a_ref[...], cols_b_ref[...])
    east_ref[...] = jnp.where(odd_col, cols_b_ref[...], cols_a_ref[...])
    wet_row = f_in_ref[FIELDS : FIELDS + 1, :]
    wet = jnp.broadcast_to(wet_row, (8, LANES))
    drift_x = jnp.broadcast_to(CURRENT_GAIN * jnp.tanh(f_in_ref[0:1, :]), (8, LANES))
    drift_y = jnp.broadcast_to(CURRENT_GAIN * jnp.tanh(f_in_ref[L : L + 1, :]), (8, LANES))

    def advect(m, carry):
        group = pl.ds(pl.multiple_of(m * 128, 128), 128)
        speed_x = jnp.broadcast_to(vectors_ref[FIELDS : FIELDS + 1, group], (128, LANES)).T
        speed_y = jnp.broadcast_to(vectors_ref[FIELDS + 1 : FIELDS + 2, group], (128, LANES)).T
        for n in range(16):
            rows = tile_rows(m * 128 + n * 8)
            tile = e_in_ref[rows, :]
            a_x = speed_x[n * 8 : n * 8 + 8] + drift_x
            a_y = speed_y[n * 8 : n * 8 + 8] + drift_y
            west, east, south, north = neighbours(tile, n, m, *halos)
            moved = (
                tile
                - jnp.maximum(a_x, 0.0) * (tile - west)
                - jnp.minimum(a_x, 0.0) * (east - tile)
                - jnp.maximum(a_y, 0.0) * (tile - south)
                - jnp.minimum(a_y, 0.0) * (north - tile)
            )
            e_ref[rows, :] = moved * wet
        return carry

    lax.fori_loop(0, channels // 128, advect, 0)

    sub = lax.broadcasted_iota(jnp.int32, (8, LANES), 0)
    here = [sub == s for s in range(8)]

    def gathered(quad):
        picked = []
        for j in range(4):
            rows = None
            for s in range(8):
                row = e_ref[pl.ds(index_ref[j, quad + s], 8, stride=0), :]
                rows = row if rows is None else jnp.where(here[s], row, rows)
            picked.append(rows)
        first, second, third, fourth = picked
        return first * second * (third + fourth) - third * fourth * (first + second)

    def substep(_, carry):
        for quad in range(0, quads, 16):
            both = jnp.concatenate([gathered(quad), gathered(quad + 8)], axis=0)
            inter_ref[quad : quad + 16, :] = both.astype(jnp.bfloat16)
        growth = jnp.dot(coupling_ref[...], inter_ref[...], preferred_element_type=jnp.float32)
        gained = SOURCE_GAIN * growth / (1.0 + SOURCE_GAIN * jnp.abs(growth))
        e_ref[0:channels, :] = e_ref[0:channels, :] + wet_row * gained
        return carry

    lax.fori_loop(0, SUB, substep, 0)

    energy = e_ref[0:channels, :]
    e_out_ref[...] = energy
    stokes = jnp.dot(
        vectors_ref[0:FIELDS, :], energy, precision=lax.Precision.HIGHEST, preferred_element_type=jnp.float32
    )

    tiles = [f_in_ref[n * 8 : n * 8 + 8, :] for n in range(FIELDS // 8)]
    around = [neighbours(tile, n, channels // 128, *halos) for n, tile in enumerate(tiles)]
    half = L // 8
    level = lax.broadcasted_iota(jnp.int32, (L, LANES), 0)

    def field(lo):
        whole = jnp.concatenate(tiles[lo : lo + half], axis=0)
        sides = [jnp.concatenate([around[n][d] for n in range(lo, lo + half)], axis=0) for d in range(4)]
        above = jnp.where(level == 0, 0.0, roll(whole, 1, 0))
        below = jnp.where(level == L - 1, 0.0, roll(whole, -1, 0))
        mixed = VISCOSITY * (sides[1] + sides[0] + sides[3] + sides[2] - 4.0 * whole) + MIXING * (
            below + above - 2.0 * whole
        )
        return whole, sides, mixed

    flow_x, sides_x, mixed_x = field(0)
    flow_y, sides_y, mixed_y = field(half)
    vortex = 0.5 * (sides_y[1] - sides_y[0]) - 0.5 * (sides_x[3] - sides_x[2])
    stokes_x = stokes[0:L]
    stokes_y = stokes[L : 2 * L]
    f_out_ref[0:L, :] = flow_x + CORIOLIS * (flow_y + stokes_y) + vortex * stokes_y + mixed_x
    f_out_ref[L : 2 * L, :] = flow_y - CORIOLIS * (flow_x + stokes_x) - vortex * stokes_x + mixed_y

    if not last:
        f_out_ref[FIELDS:, :] = f_in_ref[FIELDS:, :]
        pack_all(e_ref, f_out_ref, channels, edges)


def exchange(values, axis):
    peers = lax.axis_size(axis)
    lines = values.reshape(peers, 1, values.size // peers)
    moved = lax.all_to_all(lines, axis, split_axis=0, concat_axis=0, tiled=True)
    return moved.reshape(values.shape)


def swap_edges(edges):
    rows_a, rows_b, cols_a, cols_b = edges

    def swap(value, axis, shift):
        count = lax.axis_size(axis)
        partner = [((i + shift) ^ 1) - shift for i in range(count)]
        return lax.ppermute(value, axis, [(i, j) for i, j in enumerate(partner) if 0 <= j < count])

    from_b = swap(rows_b, "grp", 1)
    from_a = swap(rows_a, "grp", 0)
    return (from_a, from_b, swap(cols_b, "comp", 1), swap(cols_a, "comp", 0))


def local(spectrum, group_speed, sea_mask, quad_index, coupling, stokes_kernel, ocean_flow):
    parts, rows_local, columns = spectrum.shape
    cols_local = ocean_flow.shape[3]
    peers = columns // cols_local
    groups = ocean_flow.shape[2] // rows_local
    channels = parts * peers
    quads = quad_index.shape[1]
    comp_place = lax.axis_index("comp")
    group_place = lax.axis_index("grp")

    float_of = lambda *shape: jax.ShapeDtypeStruct(shape, jnp.float32)
    edge_shapes = [float_of((channels // 64 + 1) * 8, LANES)] * 2 + [
        float_of((channels // 128 + 1) * 8, LANES)
    ] * 2

    wet_rows = (sea_mask == 1).astype(jnp.float32)
    wet = lax.dynamic_slice_in_dim(wet_rows, comp_place * cols_local, cols_local, 1).reshape(1, LANES)
    flow = lax.dynamic_slice_in_dim(ocean_flow, group_place * rows_local, rows_local, 2).reshape(FIELDS, LANES)
    flow = jnp.concatenate([flow, wet, jnp.zeros((7, LANES), jnp.float32)], axis=0)

    vectors = jnp.concatenate([stokes_kernel, group_speed, jnp.zeros((6, channels), jnp.float32)], axis=0)

    blocks = columns // LANES
    sent = pl.pallas_call(
        to_points_kernel,
        out_shape=float_of(channels, LANES),
        in_specs=[HBM],
        out_specs=HBM,
        scratch_shapes=[
            pltpu.VMEM(spectrum.shape, jnp.float32),
            pltpu.VMEM((channels, LANES), jnp.float32),
            pltpu.SemaphoreType.DMA((blocks,)),
            pltpu.SemaphoreType.DMA((blocks,)),
        ],
        name="to_points",
    )(spectrum)
    energy, flow, vectors = lax.optimization_barrier((exchange(sent, "comp"), flow, vectors))
    edges = pl.pallas_call(
        edges_kernel, out_shape=edge_shapes, in_specs=[VMEM] * 2, out_specs=[VMEM] * 4, compiler_params=SMALL, name="edges"
    )(energy, flow)
    for iteration in range(STEPS):
        last = iteration == STEPS - 1
        from_a, from_b, from_cols_b, from_cols_a = swap_edges(edges)
        outs = [float_of(channels, LANES), float_of(FIELDS if last else FIELDS + 8, LANES)] + ([] if last else edge_shapes)
        energy, flow, *edges = pl.pallas_call(
            functools.partial(step_kernel, last),
            out_shape=outs,
            in_specs=[SMEM] + [VMEM] * 8,
            out_specs=[VMEM] * len(outs),
            scratch_shapes=[
                pltpu.VMEM((channels + 8, LANES), jnp.float32),
                pltpu.VMEM((quads, LANES), jnp.bfloat16),
            ]
            + [pltpu.VMEM(edge.shape, jnp.float32) for edge in edge_shapes],
            compiler_params=STEP,
            name="last_step" if last else "step",
        )(quad_index, energy, flow, vectors, coupling, from_a, from_b, from_cols_a, from_cols_b)
    half = groups // 2
    near = [lax.ppermute(flow, "grp", [(i, i ^ by) for i in range(groups)]) for by in range(1, half)]
    energy, *tiles = lax.optimization_barrier((energy, flow, *near))
    returned = exchange(energy, "comp")
    forecast = pl.pallas_call(
        from_points_kernel,
        out_shape=float_of(parts, rows_local, columns),
        in_specs=[VMEM],
        out_specs=HBM,
        scratch_shapes=[pltpu.VMEM(spectrum.shape, jnp.float32), pltpu.SemaphoreType.DMA((blocks,))],
        compiler_params=SMALL,
        name="from_points",
    )(returned)
    bit = 1
    while bit < half:
        upper = (group_place & bit) != 0
        tiles = [jnp.where(upper, tiles[j ^ bit], tiles[j]) for j in range(half)]
        bit *= 2
    held = jnp.stack(tiles)
    far = lax.ppermute(held, "grp", [(i, i ^ half) for i in range(groups)])
    upper = (group_place & half) != 0
    fields = jnp.stack([jnp.where(upper, far, held), jnp.where(upper, held, far)])
    fields = fields.reshape(groups, 2, L, rows_local, cols_local)
    ocean = fields.transpose(1, 2, 0, 3, 4).reshape(2, L, groups * rows_local, cols_local)
    return forecast, ocean


def solution(mesh):
    in_specs = (
        P("comp", "grp", None),
        P(),
        P("grp", None),
        P(),
        P(),
        P(),
        P(None, None, None, "comp"),
    )
    out_specs = (P("comp", "grp", None), P(None, None, None, "comp"))
    return jax.shard_map(local, mesh=mesh, in_specs=in_specs, out_specs=out_specs, check_vma=False)
```

```python
import functools

import jax
import jax.numpy as jnp
from jax import lax
from jax.experimental import pallas as pl
from jax.experimental.pallas import tpu as pltpu
from jax.sharding import PartitionSpec as P

L = 16
STEPS = 2
SUB = 3

SOURCE_GAIN = 0.3
CURRENT_GAIN = 0.25
CORIOLIS = 0.3
VISCOSITY = 0.15
MIXING = 0.15

ROWS = 8
COLS = 16
LANES = 128
FIELDS = 2 * L

VMEM = pl.BlockSpec(memory_space=pltpu.VMEM)
SMEM = pl.BlockSpec(memory_space=pltpu.SMEM)
HBM = pl.BlockSpec(memory_space=pltpu.HBM)
STEP = pltpu.CompilerParams(vmem_limit_bytes=16 * 2**20)
SMALL = pltpu.CompilerParams(vmem_limit_bytes=16 * 2**20)


def roll(x, shift, axis=1):
    shift %= x.shape[axis]
    return pltpu.roll(x, shift, axis) if shift else x


def lane_places():
    lane = lax.broadcasted_iota(jnp.int32, (8, LANES), 1)
    return lane // COLS, lane % COLS


def exchange_blocks(x):
    sub = lax.broadcasted_iota(jnp.int32, (8, LANES), 0)
    block, _ = lane_places()
    for bit in (1, 2, 4):
        in_sub = (sub & bit) != 0
        in_block = (block & bit) != 0
        up = roll(roll(x, -bit, 0), bit * COLS)
        down = roll(roll(x, bit, 0), -bit * COLS)
        x = jnp.where(in_sub == in_block, x, jnp.where(in_block, up, down))
    return x


def to_points_kernel(x_ref, o_ref):
    parts = x_ref.shape[0]

    def one(k, carry):
        for j in range(x_ref.shape[2] // LANES):
            tile = exchange_blocks(x_ref[k, :, j * LANES : (j + 1) * LANES])
            o_ref[pl.ds(j * 8 * parts + k, 8, stride=parts), :] = tile
        return carry

    lax.fori_loop(0, parts, one, 0, unroll=3)


def from_points_kernel(x_ref, o_ref):
    parts = o_ref.shape[0]

    def one(k, carry):
        for j in range(o_ref.shape[2] // LANES):
            tile = x_ref[pl.ds(j * 8 * parts + k, 8, stride=parts), :]
            o_ref[k, :, j * LANES : (j + 1) * LANES] = exchange_blocks(tile)
        return carry

    lax.fori_loop(0, parts, one, 0, unroll=3)


def tile_rows(start, count=8):
    return pl.ds(start if isinstance(start, int) else pl.multiple_of(start, 8), count)


def parities():
    return lax.axis_index("grp") % 2 == 1, lax.axis_index("comp") % 2 == 1


def pack_group(load, count, m, rows_a_ref, rows_b_ref, cols_a_ref, cols_b_ref):
    odd_row, odd_col = parities()
    block, col = lane_places()
    east = west = None
    for h in range((count + 7) // 8):
        up = down = None
        for i in range(min(8, count - 8 * h)):
            n = 8 * h + i
            tile = load(n)
            u = roll(tile, (i - (ROWS - 1)) * COLS)
            d = roll(tile, i * COLS)
            e = roll(tile, n - (COLS - 1))
            w = roll(tile, n)
            up = u if up is None else jnp.where(block == i, u, up)
            down = d if down is None else jnp.where(block == i, d, down)
            east = e if east is None else jnp.where(col == n, e, east)
            west = w if west is None else jnp.where(col == n, w, west)
        rows_a_ref[tile_rows((2 * m + h) * 8), :] = jnp.where(odd_row, down, up)
        rows_b_ref[tile_rows((2 * m + h) * 8), :] = jnp.where(odd_row, up, down)
    cols_a_ref[tile_rows(m * 8), :] = jnp.where(odd_col, west, east)
    cols_b_ref[tile_rows(m * 8), :] = jnp.where(odd_col, east, west)


def pack_all(e_ref, f_ref, channels, edges):
    def one(m, carry):
        pack_group(lambda n: e_ref[tile_rows(m * 128 + n * 8), :], 16, m, *edges)
        return carry

    lax.fori_loop(0, channels // 128, one, 0)
    pack_group(lambda n: f_ref[n * 8 : n * 8 + 8, :], FIELDS // 8, channels // 128, *edges)


def neighbours(tile, n, m, south_ref, north_ref, west_ref, east_ref):
    block, col = lane_places()
    h, i = divmod(n, 8)
    south = roll(south_ref[tile_rows((2 * m + h) * 8), :], -i * COLS)
    north = roll(north_ref[tile_rows((2 * m + h) * 8), :], (ROWS - 1 - i) * COLS)
    west = roll(west_ref[tile_rows(m * 8), :], -n)
    east = roll(east_ref[tile_rows(m * 8), :], COLS - 1 - n)
    return (
        jnp.where(col == 0, west, roll(tile, 1)),
        jnp.where(col == COLS - 1, east, roll(tile, -1)),
        jnp.where(block == 0, south, roll(tile, COLS)),
        jnp.where(block == ROWS - 1, north, roll(tile, -COLS)),
    )


def edges_kernel(e_ref, f_ref, *edges):
    pack_all(e_ref, f_ref, e_ref.shape[0], edges)


def step_kernel(
    last,
    index_ref,
    e_in_ref,
    f_in_ref,
    vectors_ref,
    coupling_ref,
    rows_a_ref,
    rows_b_ref,
    cols_a_ref,
    cols_b_ref,
    e_out_ref,
    f_out_ref,
    *rest,
):
    edges, (e_ref, inter_ref, *halos) = rest[:-6], rest[-6:]
    channels = e_in_ref.shape[0]
    quads = inter_ref.shape[0]
    odd_row, odd_col = parities()
    south_ref, north_ref, west_ref, east_ref = halos
    south_ref[...] = jnp.where(odd_row, rows_a_ref[...], rows_b_ref[...])
    north_ref[...] = jnp.where(odd_row, rows_b_ref[...], rows_a_ref[...])
    west_ref[...] = jnp.where(odd_col, cols_a_ref[...], cols_b_ref[...])
    east_ref[...] = jnp.where(odd_col, cols_b_ref[...], cols_a_ref[...])
    wet_row = f_in_ref[FIELDS : FIELDS + 1, :]
    wet = jnp.broadcast_to(wet_row, (8, LANES))
    drift_x = jnp.broadcast_to(CURRENT_GAIN * jnp.tanh(f_in_ref[0:1, :]), (8, LANES))
    drift_y = jnp.broadcast_to(CURRENT_GAIN * jnp.tanh(f_in_ref[L : L + 1, :]), (8, LANES))

    def advect(m, carry):
        group = pl.ds(pl.multiple_of(m * 128, 128), 128)
        speed_x = jnp.broadcast_to(vectors_ref[FIELDS : FIELDS + 1, group], (128, LANES)).T
        speed_y = jnp.broadcast_to(vectors_ref[FIELDS + 1 : FIELDS + 2, group], (128, LANES)).T
        for n in range(16):
            rows = tile_rows(m * 128 + n * 8)
            tile = e_in_ref[rows, :]
            a_x = speed_x[n * 8 : n * 8 + 8] + drift_x
            a_y = speed_y[n * 8 : n * 8 + 8] + drift_y
            west, east, south, north = neighbours(tile, n, m, *halos)
            moved = (
                tile
                - jnp.maximum(a_x, 0.0) * (tile - west)
                - jnp.minimum(a_x, 0.0) * (east - tile)
                - jnp.maximum(a_y, 0.0) * (tile - south)
                - jnp.minimum(a_y, 0.0) * (north - tile)
            )
            e_ref[rows, :] = moved * wet
        return carry

    lax.fori_loop(0, channels // 128, advect, 0)

    sub = lax.broadcasted_iota(jnp.int32, (8, LANES), 0)
    here = [sub == s for s in range(8)]

    def gathered(quad):
        picked = []
        for j in range(4):
            rows = None
            for s in range(8):
                row = e_ref[pl.ds(index_ref[j, quad + s], 8, stride=0), :]
                rows = row if rows is None else jnp.where(here[s], row, rows)
            picked.append(rows)
        first, second, third, fourth = picked
        return first * second * (third + fourth) - third * fourth * (first + second)

    def substep(_, carry):
        for quad in range(0, quads, 16):
            both = jnp.concatenate([gathered(quad), gathered(quad + 8)], axis=0)
            inter_ref[quad : quad + 16, :] = both.astype(jnp.bfloat16)
        growth = jnp.dot(coupling_ref[...], inter_ref[...], preferred_element_type=jnp.float32)
        gained = SOURCE_GAIN * growth / (1.0 + SOURCE_GAIN * jnp.abs(growth))
        e_ref[0:channels, :] = e_ref[0:channels, :] + wet_row * gained
        return carry

    lax.fori_loop(0, SUB, substep, 0)

    energy = e_ref[0:channels, :]
    e_out_ref[...] = energy
    stokes = jnp.dot(
        vectors_ref[0:FIELDS, :], energy, precision=lax.Precision.HIGHEST, preferred_element_type=jnp.float32
    )

    tiles = [f_in_ref[n * 8 : n * 8 + 8, :] for n in range(FIELDS // 8)]
    around = [neighbours(tile, n, channels // 128, *halos) for n, tile in enumerate(tiles)]
    half = L // 8
    level = lax.broadcasted_iota(jnp.int32, (L, LANES), 0)

    def field(lo):
        whole = jnp.concatenate(tiles[lo : lo + half], axis=0)
        sides = [jnp.concatenate([around[n][d] for n in range(lo, lo + half)], axis=0) for d in range(4)]
        above = jnp.where(level == 0, 0.0, roll(whole, 1, 0))
        below = jnp.where(level == L - 1, 0.0, roll(whole, -1, 0))
        mixed = VISCOSITY * (sides[1] + sides[0] + sides[3] + sides[2] - 4.0 * whole) + MIXING * (
            below + above - 2.0 * whole
        )
        return whole, sides, mixed

    flow_x, sides_x, mixed_x = field(0)
    flow_y, sides_y, mixed_y = field(half)
    vortex = 0.5 * (sides_y[1] - sides_y[0]) - 0.5 * (sides_x[3] - sides_x[2])
    stokes_x = stokes[0:L]
    stokes_y = stokes[L : 2 * L]
    f_out_ref[0:L, :] = flow_x + CORIOLIS * (flow_y + stokes_y) + vortex * stokes_y + mixed_x
    f_out_ref[L : 2 * L, :] = flow_y - CORIOLIS * (flow_x + stokes_x) - vortex * stokes_x + mixed_y

    if not last:
        f_out_ref[FIELDS:, :] = f_in_ref[FIELDS:, :]
        pack_all(e_ref, f_out_ref, channels, edges)


def exchange(values, axis):
    peers = lax.axis_size(axis)
    lines = values.reshape(peers, 1, values.size // peers)
    moved = lax.all_to_all(lines, axis, split_axis=0, concat_axis=0, tiled=True)
    return moved.reshape(values.shape)


def swap_edges(edges):
    rows_a, rows_b, cols_a, cols_b = edges

    def swap(value, axis, shift):
        count = lax.axis_size(axis)
        partner = [((i + shift) ^ 1) - shift for i in range(count)]
        return lax.ppermute(value, axis, [(i, j) for i, j in enumerate(partner) if 0 <= j < count])

    from_b = swap(rows_b, "grp", 1)
    from_a = swap(rows_a, "grp", 0)
    return (from_a, from_b, swap(cols_b, "comp", 1), swap(cols_a, "comp", 0))


def local(spectrum, group_speed, sea_mask, quad_index, coupling, stokes_kernel, ocean_flow):
    parts, rows_local, columns = spectrum.shape
    cols_local = ocean_flow.shape[3]
    peers = columns // cols_local
    groups = ocean_flow.shape[2] // rows_local
    channels = parts * peers
    quads = quad_index.shape[1]
    comp_place = lax.axis_index("comp")
    group_place = lax.axis_index("grp")

    float_of = lambda *shape: jax.ShapeDtypeStruct(shape, jnp.float32)
    edge_shapes = [float_of((channels // 64 + 1) * 8, LANES)] * 2 + [
        float_of((channels // 128 + 1) * 8, LANES)
    ] * 2

    wet_rows = (sea_mask == 1).astype(jnp.float32)
    wet = lax.dynamic_slice_in_dim(wet_rows, comp_place * cols_local, cols_local, 1).reshape(1, LANES)
    flow = lax.dynamic_slice_in_dim(ocean_flow, group_place * rows_local, rows_local, 2).reshape(FIELDS, LANES)
    flow = jnp.concatenate([flow, wet, jnp.zeros((7, LANES), jnp.float32)], axis=0)

    vectors = jnp.concatenate([stokes_kernel, group_speed, jnp.zeros((6, channels), jnp.float32)], axis=0)

    sent = pl.pallas_call(
        to_points_kernel, out_shape=float_of(channels, LANES), in_specs=[VMEM], out_specs=VMEM, compiler_params=SMALL, name="to_points"
    )(spectrum)
    energy, flow, vectors = lax.optimization_barrier((exchange(sent, "comp"), flow, vectors))
    edges = pl.pallas_call(
        edges_kernel, out_shape=edge_shapes, in_specs=[VMEM] * 2, out_specs=[VMEM] * 4, compiler_params=SMALL, name="edges"
    )(energy, flow)
    for iteration in range(STEPS):
        last = iteration == STEPS - 1
        from_a, from_b, from_cols_b, from_cols_a = swap_edges(edges)
        outs = [float_of(channels, LANES), float_of(FIELDS if last else FIELDS + 8, LANES)] + ([] if last else edge_shapes)
        energy, flow, *edges = pl.pallas_call(
            functools.partial(step_kernel, last),
            out_shape=outs,
            in_specs=[SMEM] + [VMEM] * 8,
            out_specs=[VMEM] * len(outs),
            scratch_shapes=[
                pltpu.VMEM((channels + 8, LANES), jnp.float32),
                pltpu.VMEM((quads, LANES), jnp.bfloat16),
            ]
            + [pltpu.VMEM(edge.shape, jnp.float32) for edge in edge_shapes],
            compiler_params=STEP,
            name="last_step" if last else "step",
        )(quad_index, energy, flow, vectors, coupling, from_a, from_b, from_cols_a, from_cols_b)
    returned = exchange(energy, "comp")
    half = groups // 2
    far = lax.ppermute(flow, "grp", [(i, i ^ half) for i in range(groups)])
    upper = (group_place & half) != 0
    held = jnp.stack([jnp.where(upper, far, flow), jnp.where(upper, flow, far)])
    tiles = [held] + [lax.ppermute(held, "grp", [(i, i ^ by) for i in range(groups)]) for by in range(1, half)]
    forecast = pl.pallas_call(
        from_points_kernel,
        out_shape=float_of(parts, rows_local, columns),
        in_specs=[VMEM],
        out_specs=VMEM,
        compiler_params=SMALL,
        name="from_points",
    )(returned)
    bit = 1
    while bit < half:
        upper = (group_place & bit) != 0
        tiles = [jnp.where(upper, tiles[j ^ bit], tiles[j]) for j in range(half)]
        bit *= 2
    fields = jnp.stack(tiles).reshape(half, 2, 2, L, rows_local, cols_local)
    ocean = fields.transpose(2, 3, 1, 0, 4, 5).reshape(2, L, groups * rows_local, cols_local)
    return forecast, ocean


def solution(mesh):
    in_specs = (
        P("comp", "grp", None),
        P(),
        P("grp", None),
        P(),
        P(),
        P(),
        P(None, None, None, "comp"),
    )
    out_specs = (P("comp", "grp", None), P(None, None, None, "comp"))
    return jax.shard_map(local, mesh=mesh, in_specs=in_specs, out_specs=out_specs, check_vma=False)
```

```python
import functools

import jax
import jax.numpy as jnp
from jax import lax
from jax.experimental import pallas as pl
from jax.experimental.pallas import tpu as pltpu
from jax.sharding import PartitionSpec as P

L = 16
STEPS = 2
SUB = 3

SOURCE_GAIN = 0.3
CURRENT_GAIN = 0.25
CORIOLIS = 0.3
VISCOSITY = 0.15
MIXING = 0.15

ROWS = 8
COLS = 16
LANES = 128
FIELDS = 2 * L

VMEM = pl.BlockSpec(memory_space=pltpu.VMEM)
SMEM = pl.BlockSpec(memory_space=pltpu.SMEM)
HBM = pl.BlockSpec(memory_space=pltpu.HBM)
STEP = pltpu.CompilerParams(vmem_limit_bytes=16 * 2**20)
SMALL = pltpu.CompilerParams(vmem_limit_bytes=16 * 2**20)


def roll(x, shift, axis=1):
    shift %= x.shape[axis]
    return pltpu.roll(x, shift, axis) if shift else x


def lane_places():
    lane = lax.broadcasted_iota(jnp.int32, (8, LANES), 1)
    return lane // COLS, lane % COLS


def exchange_blocks(x):
    sub = lax.broadcasted_iota(jnp.int32, (8, LANES), 0)
    block, _ = lane_places()
    for bit in (1, 2, 4):
        in_sub = (sub & bit) != 0
        in_block = (block & bit) != 0
        up = roll(roll(x, -bit, 0), bit * COLS)
        down = roll(roll(x, bit, 0), -bit * COLS)
        x = jnp.where(in_sub == in_block, x, jnp.where(in_block, up, down))
    return x


def to_points_kernel(x_ref, o_ref):
    parts = x_ref.shape[0]

    def one(k, carry):
        for j in range(x_ref.shape[2] // LANES):
            tile = exchange_blocks(x_ref[k, :, j * LANES : (j + 1) * LANES])
            o_ref[pl.ds(j * 8 * parts + k, 8, stride=parts), :] = tile
        return carry

    lax.fori_loop(0, parts, one, 0, unroll=3)


def from_points_kernel(x_ref, o_ref):
    parts = o_ref.shape[0]

    def one(k, carry):
        for j in range(o_ref.shape[2] // LANES):
            tile = x_ref[pl.ds(j * 8 * parts + k, 8, stride=parts), :]
            o_ref[k, :, j * LANES : (j + 1) * LANES] = exchange_blocks(tile)
        return carry

    lax.fori_loop(0, parts, one, 0, unroll=3)


def tile_rows(start, count=8):
    return pl.ds(start if isinstance(start, int) else pl.multiple_of(start, 8), count)


def parities():
    return lax.axis_index("grp") % 2 == 1, lax.axis_index("comp") % 2 == 1


def pack_group(load, count, m, rows_a_ref, rows_b_ref, cols_a_ref, cols_b_ref):
    odd_row, odd_col = parities()
    block, col = lane_places()
    east = west = None
    for h in range((count + 7) // 8):
        up = down = None
        for i in range(min(8, count - 8 * h)):
            n = 8 * h + i
            tile = load(n)
            u = roll(tile, (i - (ROWS - 1)) * COLS)
            d = roll(tile, i * COLS)
            e = roll(tile, n - (COLS - 1))
            w = roll(tile, n)
            up = u if up is None else jnp.where(block == i, u, up)
            down = d if down is None else jnp.where(block == i, d, down)
            east = e if east is None else jnp.where(col == n, e, east)
            west = w if west is None else jnp.where(col == n, w, west)
        rows_a_ref[tile_rows((2 * m + h) * 8), :] = jnp.where(odd_row, down, up)
        rows_b_ref[tile_rows((2 * m + h) * 8), :] = jnp.where(odd_row, up, down)
    cols_a_ref[tile_rows(m * 8), :] = jnp.where(odd_col, west, east)
    cols_b_ref[tile_rows(m * 8), :] = jnp.where(odd_col, east, west)


def pack_all(e_ref, f_ref, channels, edges):
    def one(m, carry):
        pack_group(lambda n: e_ref[tile_rows(m * 128 + n * 8), :], 16, m, *edges)
        return carry

    lax.fori_loop(0, channels // 128, one, 0)
    pack_group(lambda n: f_ref[n * 8 : n * 8 + 8, :], FIELDS // 8, channels // 128, *edges)


def neighbours(tile, n, m, south_ref, north_ref, west_ref, east_ref):
    block, col = lane_places()
    h, i = divmod(n, 8)
    south = roll(south_ref[tile_rows((2 * m + h) * 8), :], -i * COLS)
    north = roll(north_ref[tile_rows((2 * m + h) * 8), :], (ROWS - 1 - i) * COLS)
    west = roll(west_ref[tile_rows(m * 8), :], -n)
    east = roll(east_ref[tile_rows(m * 8), :], COLS - 1 - n)
    return (
        jnp.where(col == 0, west, roll(tile, 1)),
        jnp.where(col == COLS - 1, east, roll(tile, -1)),
        jnp.where(block == 0, south, roll(tile, COLS)),
        jnp.where(block == ROWS - 1, north, roll(tile, -COLS)),
    )


def edges_kernel(e_ref, f_ref, *edges):
    pack_all(e_ref, f_ref, e_ref.shape[0], edges)


def step_kernel(
    last,
    index_ref,
    e_in_ref,
    f_in_ref,
    vectors_ref,
    coupling_ref,
    rows_b_ref,
    cols_b_ref,
    rows_a_ref,
    cols_a_ref,
    e_out_ref,
    f_out_ref,
    *rest,
):
    edges, (e_ref, inter_ref, *halos) = rest[:-6], rest[-6:]
    channels = e_in_ref.shape[0]
    quads = inter_ref.shape[0]
    odd_row, odd_col = parities()
    south_ref, north_ref, west_ref, east_ref = halos
    south_ref[...] = jnp.where(odd_row, rows_a_ref[...], rows_b_ref[...])
    north_ref[...] = jnp.where(odd_row, rows_b_ref[...], rows_a_ref[...])
    west_ref[...] = jnp.where(odd_col, cols_a_ref[...], cols_b_ref[...])
    east_ref[...] = jnp.where(odd_col, cols_b_ref[...], cols_a_ref[...])
    wet_row = f_in_ref[FIELDS : FIELDS + 1, :]
    wet = jnp.broadcast_to(wet_row, (8, LANES))
    drift_x = jnp.broadcast_to(CURRENT_GAIN * jnp.tanh(f_in_ref[0:1, :]), (8, LANES))
    drift_y = jnp.broadcast_to(CURRENT_GAIN * jnp.tanh(f_in_ref[L : L + 1, :]), (8, LANES))

    def advect(m, carry):
        group = pl.ds(pl.multiple_of(m * 128, 128), 128)
        speed_x = jnp.broadcast_to(vectors_ref[FIELDS : FIELDS + 1, group], (128, LANES)).T
        speed_y = jnp.broadcast_to(vectors_ref[FIELDS + 1 : FIELDS + 2, group], (128, LANES)).T
        for n in range(16):
            rows = tile_rows(m * 128 + n * 8)
            tile = e_in_ref[rows, :]
            a_x = speed_x[n * 8 : n * 8 + 8] + drift_x
            a_y = speed_y[n * 8 : n * 8 + 8] + drift_y
            west, east, south, north = neighbours(tile, n, m, *halos)
            moved = (
                tile
                - jnp.maximum(a_x, 0.0) * (tile - west)
                - jnp.minimum(a_x, 0.0) * (east - tile)
                - jnp.maximum(a_y, 0.0) * (tile - south)
                - jnp.minimum(a_y, 0.0) * (north - tile)
            )
            e_ref[rows, :] = moved * wet
        return carry

    lax.fori_loop(0, channels // 128, advect, 0)

    sub = lax.broadcasted_iota(jnp.int32, (8, LANES), 0)
    here = [sub == s for s in range(8)]

    def gathered(quad):
        picked = []
        for j in range(4):
            rows = None
            for s in range(8):
                row = e_ref[pl.ds(index_ref[j, quad + s], 8, stride=0), :]
                rows = row if rows is None else jnp.where(here[s], row, rows)
            picked.append(rows)
        first, second, third, fourth = picked
        return first * second * (third + fourth) - third * fourth * (first + second)

    def substep(_, carry):
        for quad in range(0, quads, 16):
            both = jnp.concatenate([gathered(quad), gathered(quad + 8)], axis=0)
            inter_ref[quad : quad + 16, :] = both.astype(jnp.bfloat16)
        growth = jnp.dot(coupling_ref[...], inter_ref[...], preferred_element_type=jnp.float32)
        gained = SOURCE_GAIN * growth / (1.0 + SOURCE_GAIN * jnp.abs(growth))
        e_ref[0:channels, :] = e_ref[0:channels, :] + wet_row * gained
        return carry

    lax.fori_loop(0, SUB, substep, 0)

    energy = e_ref[0:channels, :]
    e_out_ref[...] = energy
    stokes = jnp.dot(
        vectors_ref[0:FIELDS, :], energy, precision=lax.Precision.HIGHEST, preferred_element_type=jnp.float32
    )

    tiles = [f_in_ref[n * 8 : n * 8 + 8, :] for n in range(FIELDS // 8)]
    around = [neighbours(tile, n, channels // 128, *halos) for n, tile in enumerate(tiles)]
    half = L // 8
    level = lax.broadcasted_iota(jnp.int32, (L, LANES), 0)

    def field(lo):
        whole = jnp.concatenate(tiles[lo : lo + half], axis=0)
        sides = [jnp.concatenate([around[n][d] for n in range(lo, lo + half)], axis=0) for d in range(4)]
        above = jnp.where(level == 0, 0.0, roll(whole, 1, 0))
        below = jnp.where(level == L - 1, 0.0, roll(whole, -1, 0))
        mixed = VISCOSITY * (sides[1] + sides[0] + sides[3] + sides[2] - 4.0 * whole) + MIXING * (
            below + above - 2.0 * whole
        )
        return whole, sides, mixed

    flow_x, sides_x, mixed_x = field(0)
    flow_y, sides_y, mixed_y = field(half)
    vortex = 0.5 * (sides_y[1] - sides_y[0]) - 0.5 * (sides_x[3] - sides_x[2])
    stokes_x = stokes[0:L]
    stokes_y = stokes[L : 2 * L]
    f_out_ref[0:L, :] = flow_x + CORIOLIS * (flow_y + stokes_y) + vortex * stokes_y + mixed_x
    f_out_ref[L : 2 * L, :] = flow_y - CORIOLIS * (flow_x + stokes_x) - vortex * stokes_x + mixed_y

    if not last:
        f_out_ref[FIELDS:, :] = f_in_ref[FIELDS:, :]
        pack_all(e_ref, f_out_ref, channels, edges)


def exchange(values, axis):
    peers = lax.axis_size(axis)
    lines = values.reshape(peers, 1, values.size // peers)
    moved = lax.all_to_all(lines, axis, split_axis=0, concat_axis=0, tiled=True)
    return moved.reshape(values.shape)


def swap_edges(edges):
    rows_a, rows_b, cols_a, cols_b = edges

    def swap(value, axis, shift):
        count = lax.axis_size(axis)
        partner = [((i + shift) ^ 1) - shift for i in range(count)]
        return lax.ppermute(value, axis, [(i, j) for i, j in enumerate(partner) if 0 <= j < count])

    return swap(rows_b, "grp", 1), swap(cols_b, "comp", 1), swap(rows_a, "grp", 0), swap(cols_a, "comp", 0)


def local(spectrum, group_speed, sea_mask, quad_index, coupling, stokes_kernel, ocean_flow):
    parts, rows_local, columns = spectrum.shape
    cols_local = ocean_flow.shape[3]
    peers = columns // cols_local
    groups = ocean_flow.shape[2] // rows_local
    channels = parts * peers
    quads = quad_index.shape[1]
    comp_place = lax.axis_index("comp")
    group_place = lax.axis_index("grp")

    float_of = lambda *shape: jax.ShapeDtypeStruct(shape, jnp.float32)
    edge_shapes = [float_of((channels // 64 + 1) * 8, LANES)] * 2 + [
        float_of((channels // 128 + 1) * 8, LANES)
    ] * 2

    wet_rows = (sea_mask == 1).astype(jnp.float32)
    wet = lax.dynamic_slice_in_dim(wet_rows, comp_place * cols_local, cols_local, 1).reshape(1, LANES)
    flow = lax.dynamic_slice_in_dim(ocean_flow, group_place * rows_local, rows_local, 2).reshape(FIELDS, LANES)
    flow = jnp.concatenate([flow, wet, jnp.zeros((7, LANES), jnp.float32)], axis=0)

    vectors = jnp.concatenate([stokes_kernel, group_speed, jnp.zeros((6, channels), jnp.float32)], axis=0)

    sent = pl.pallas_call(
        to_points_kernel, out_shape=float_of(channels, LANES), in_specs=[VMEM], out_specs=VMEM, compiler_params=SMALL, name="to_points"
    )(spectrum)
    energy, flow, vectors = lax.optimization_barrier((exchange(sent, "comp"), flow, vectors))
    edges = pl.pallas_call(
        edges_kernel, out_shape=edge_shapes, in_specs=[VMEM] * 2, out_specs=[VMEM] * 4, compiler_params=SMALL, name="edges"
    )(energy, flow)
    for iteration in range(STEPS):
        last = iteration == STEPS - 1
        outs = [float_of(channels, LANES), float_of(FIELDS if last else FIELDS + 8, LANES)] + ([] if last else edge_shapes)
        energy, flow, *edges = pl.pallas_call(
            functools.partial(step_kernel, last),
            out_shape=outs,
            in_specs=[SMEM] + [VMEM] * 8,
            out_specs=[VMEM] * len(outs),
            scratch_shapes=[
                pltpu.VMEM((channels + 8, LANES), jnp.float32),
                pltpu.VMEM((quads, LANES), jnp.bfloat16),
            ]
            + [pltpu.VMEM(edge.shape, jnp.float32) for edge in edge_shapes],
            compiler_params=STEP,
            name="last_step" if last else "step",
        )(quad_index, energy, flow, vectors, coupling, *swap_edges(edges))
    returned = exchange(energy, "comp")
    half = groups // 2
    far = lax.ppermute(flow, "grp", [(i, i ^ half) for i in range(groups)])
    upper = (group_place & half) != 0
    held = jnp.stack([jnp.where(upper, far, flow), jnp.where(upper, flow, far)])
    tiles = [held] + [lax.ppermute(held, "grp", [(i, i ^ by) for i in range(groups)]) for by in range(1, half)]
    forecast = pl.pallas_call(
        from_points_kernel,
        out_shape=float_of(parts, rows_local, columns),
        in_specs=[VMEM],
        out_specs=VMEM,
        compiler_params=SMALL,
        name="from_points",
    )(returned)
    bit = 1
    while bit < half:
        upper = (group_place & bit) != 0
        tiles = [jnp.where(upper, tiles[j ^ bit], tiles[j]) for j in range(half)]
        bit *= 2
    fields = jnp.stack(tiles).reshape(half, 2, 2, L, rows_local, cols_local)
    ocean = fields.transpose(2, 3, 1, 0, 4, 5).reshape(2, L, groups * rows_local, cols_local)
    return forecast, ocean


def solution(mesh):
    in_specs = (
        P("comp", "grp", None),
        P(),
        P("grp", None),
        P(),
        P(),
        P(),
        P(None, None, None, "comp"),
    )
    out_specs = (P("comp", "grp", None), P(None, None, None, "comp"))
    return jax.shard_map(local, mesh=mesh, in_specs=in_specs, out_specs=out_specs, check_vma=False)
```
